32 devices in a mesh: expert: 8 (over z, core), group: 4 (over y, x).
Axes of the slice: x: 2, y: 2, z: 4, core: 2. Of those that a mesh axis runs over, the one named last changes fastest.
Arguments:
- tokens_in: bfloat16 [4096, 2048], P(('expert', 'group')), may hold values from -6 to 6
- hidden_grad: bfloat16 [4096, 256], P(('expert', 'group')), may hold values from -3 to 3
- routing: int32 [4096], P(('expert', 'group')), may hold values from 0 to 7, as said below
- gate_up: bfloat16 [8, 2048, 512], P('expert'), may hold values from -0.125 to 0.125
Outputs:
- tokens_grad: bfloat16 [4096, 2048], P(('expert', 'group'))
- gate_up_grad: float32 [8, 2048, 512], P('expert', 'group')
The draws below stay inside these ranges and needn't reach their ends.
Inputs may be any that keep to these rules, and one draw needn't show every extreme that they name: `routing`: the 128 rows of one device (block b of the rows, b = expert index * 4 + group index) name each expert at most 32 times. Blocks b and b + 2, for b % 4 < 2, together name each expert at most 3 * 32 // 2 times. In every draw both bounds are reached, and some expert receives 32 rows from every block of one group.
All inputs are finite; a program needn't handle non-finite values.
Results may differ from the reference program's by a relative error of at most 0.0049.
Values may be sent and summed in bfloat16 or wider, within the bound.
No kernel may reach another device: no remote copies, remote signals or barrier semaphores. Data moves between devices by JAX's collectives and lax.ppermute only.
A program may use at most 64 MiB of HBM per device.

```python
import jax
import jax.numpy as jnp
from jax import lax

D = 2048
FF = 256
ROWS = 128
EXPERTS = 8
GROUPS = 4
CAP = 32
WORK = 192
HOT = 1
TOKENS = 4096


def device_routing(key, source_index, group_index):
    half_groups = GROUPS // 2
    pair_key = jax.random.fold_in(jax.random.fold_in(key, 7), group_index % half_groups)
    upper_half = group_index // half_groups
    shuffled = jax.random.permutation(pair_key, EXPERTS)
    is_hot = jnp.zeros((EXPERTS,), jnp.int32).at[shuffled[:HOT]].set(1)
    flip_bits = jax.random.randint(jax.random.fold_in(pair_key, 1), (EXPERTS,), 0, 2)
    hot_counts = is_hot * jnp.where(flip_bits == upper_half, CAP, CAP // 2)
    needed = ROWS - jnp.sum(hot_counts)
    per_expert = 3 * CAP // 4
    slot_total = EXPERTS * per_expert
    device_key = jax.random.fold_in(jax.random.fold_in(key, 11), source_index * GROUPS + group_index)
    scores = jax.random.randint(device_key, (slot_total,), 0, 1 << 20) * slot_total
    scores = scores + jnp.arange(slot_total, dtype=jnp.int32)
    slot_owner = jnp.arange(slot_total, dtype=jnp.int32) // per_expert
    scores = jnp.where(is_hot[slot_owner] == 1, -1, scores)
    ranking = jnp.argsort(jnp.argsort(-scores, stable=True), stable=True)
    chosen = (ranking < needed).astype(jnp.int32)
    counts = hot_counts + jnp.sum(chosen.reshape(EXPERTS, per_expert), axis=1)
    row_ends = jnp.cumsum(counts)
    expert_of = jnp.sum((row_ends[None, :] <= jnp.arange(ROWS, dtype=jnp.int32)[:, None]).astype(jnp.int32), axis=1)
    row_order = jax.random.permutation(jax.random.fold_in(device_key, 3), ROWS)
    return expert_of[row_order].astype(jnp.int32)


def draw_routing(key, part):

    def per_source(source_index):

        def per_group(group_index):
            return device_routing(key, source_index, group_index)
        return jax.vmap(per_group)(jnp.arange(GROUPS, dtype=jnp.int32))
    routed = jax.vmap(per_source)(jnp.arange(EXPERTS, dtype=jnp.int32))
    return routed.reshape(-1)


def levels(key, dims, shards, smallest, high):
    def one(dim, shards_of):
        heights = jax.random.uniform(jax.random.fold_in(jax.random.fold_in(key, 6), dim), (shards_of,), jnp.float32, smallest / len(shards), high / len(shards))
        return jnp.repeat(jnp.exp(heights), dims[dim] // shards_of).reshape((-1,) + (1,) * (len(dims) - dim - 1))

    level = one(*shards[0])
    for cut in shards[1:]:
        level = level * one(*cut)
    return level


def centred(own_key, dims, spread, limit, split=(), kind=jnp.bfloat16):
    loudness = levels(own_key, dims, split, -0.22, 0.18) if split else 1.0
    entries = jax.random.normal(own_key, dims, jnp.float32) * spread * loudness
    return jnp.minimum(jnp.maximum(entries, -limit), limit).astype(kind)


def setup_inputs(seed: int = 0) -> dict:
    key_of = jax.random.split(jax.random.key(seed), 5)
    tokens_in = centred(key_of[0], (TOKENS, D), 1.0, 6.0, ((0, 32),))
    hidden_grad = centred(key_of[1], (TOKENS, FF), 0.5, 3.0, ((0, 32),))
    routing = draw_routing(jax.random.fold_in(key_of[4], 71), 0)
    gate_up = centred(key_of[3], (EXPERTS, D, 2 * FF), D ** -0.5, 0.125, ((0, 8),))
    return {"tokens_in": tokens_in, "hidden_grad": hidden_grad, "routing": routing, "gate_up": gate_up}


def reference(tokens_in, hidden_grad, routing, gate_up):
    row_total = routing.shape[0]
    one_hot = (routing[:, None] == jnp.arange(EXPERTS, dtype=jnp.int32)[None, :]).astype(jnp.int32)
    before = jnp.cumsum(one_hot, axis=0) - one_hot
    position = jnp.sum(before * one_hot, axis=1).astype(jnp.int32)
    row_limit = GROUPS * WORK
    row_table = jnp.full((EXPERTS, row_limit), row_total, jnp.int32)
    row_table = row_table.at[routing, position].set(jnp.arange(row_total, dtype=jnp.int32))
    joined = jnp.concatenate([tokens_in, hidden_grad], axis=1)
    joined = jnp.concatenate([joined, jnp.zeros((1, joined.shape[1]), joined.dtype)], axis=0)

    def per_expert(pair_args):
        table_row, weights = pair_args
        rows_in = joined[table_row]
        inputs = rows_in[:, :D]
        cotangent = rows_in[:, D:].astype(jnp.float32)
        projected = jnp.dot(inputs, weights, preferred_element_type=jnp.float32)
        gate_pre = projected[:, :FF]
        up_pre = projected[:, FF:]
        sigmoid_gate = jax.nn.sigmoid(gate_pre)
        gate_grad = cotangent * up_pre * sigmoid_gate * (1.0 + gate_pre * (1.0 - sigmoid_gate))
        up_grad = cotangent * gate_pre * sigmoid_gate
        pre_grad = jnp.concatenate([gate_grad, up_grad], axis=1).astype(jnp.bfloat16)
        input_grad = lax.dot_general(pre_grad, weights, (((1,), (1,)), ((), ())),
                                     preferred_element_type=jnp.float32).astype(jnp.bfloat16)
        weight_grad = lax.dot_general(inputs, pre_grad, (((0,), (0,)), ((), ())),
                                      preferred_element_type=jnp.float32)
        return weight_grad, input_grad

    weight_grads, input_grads = lax.map(per_expert, (row_table, gate_up))
    tokens_grad = jnp.zeros((row_total + 1, D), jnp.bfloat16)
    tokens_grad = tokens_grad.at[row_table.reshape(-1)].set(input_grads.reshape(-1, D))
    return tokens_grad[:row_total], weight_grads
```

```python
import functools

import jax
import jax.numpy as jnp
from jax import lax
from jax.experimental import pallas as pl
from jax.experimental.pallas import tpu as pltpu
from jax.sharding import PartitionSpec as P


BF16 = jnp.bfloat16
F32 = jnp.float32
VMEM = pl.BlockSpec(memory_space=pltpu.VMEM)


def chunks(total, width):
    return [(at, min(width, total - at)) for at in range(0, total, width)]


def dot(a, b):
    return jnp.dot(a, b, preferred_element_type=F32)


def dot_t(a, b):
    return lax.dot_general(a, b, (((0,), (0,)), ((), ())), preferred_element_type=F32)


def dot_nt(a, b):
    return lax.dot_general(a, b, (((1,), (1,)), ((), ())), preferred_element_type=F32)


def dispatch_kernel(experts, relative, routing_ref, tokens_ref, hidden_ref, select_ref, *piece_refs):
    rows = routing_ref.shape[1]
    slots = select_ref.shape[0]
    block = routing_ref[...]
    if relative:
        block = block ^ lax.axis_index("expert").astype(jnp.int32)
    one_hot = block == lax.broadcasted_iota(jnp.int32, (experts, rows), 0)
    ones = jnp.where(one_hot, 1.0, 0.0)
    before = lax.broadcasted_iota(jnp.int32, (rows, rows), 0) < lax.broadcasted_iota(
        jnp.int32, (rows, rows), 1
    )
    ranks = dot(ones.astype(BF16), jnp.where(before, 1.0, 0.0).astype(BF16))
    rank = jnp.sum(ranks * ones, axis=0, keepdims=True).astype(jnp.int32)
    target = block * (slots // experts) + rank
    select = jnp.where(
        target == lax.broadcasted_iota(jnp.int32, (slots, rows), 0), 1.0, 0.0
    ).astype(BF16)
    select_ref[...] = select
    width = tokens_ref.shape[1]
    for source, base in ((tokens_ref, 0), (hidden_ref, width)):
        for at, size in chunks(source.shape[1], 256):
            placed = dot(select, source[:, at : at + size]).astype(BF16)
            start = 0
            for piece in piece_refs:
                end = start + piece.shape[0]
                piece[:, base + at : base + at + size] = placed[start:end]
                start = end


def expert_kernel(groups, piece_count, *refs):
    pieces = refs[:piece_count]
    weights_ref = refs[piece_count]
    grads = refs[piece_count + 1 : 2 * piece_count + 1]
    send_a, keep_a, send_b, keep_b, inputs_ref, pre_ref = refs[2 * piece_count + 1 :]
    width, hidden2 = weights_ref.shape
    hidden = hidden2 // 2
    slots = inputs_ref.shape[0]
    cotangents = []
    start = 0
    for piece in pieces:
        end = start + piece.shape[0]
        inputs_ref[start:end, :] = piece[:, :width]
        start = end
    cotangent = jnp.concatenate([piece[:, width:].astype(F32) for piece in pieces], axis=0)
    projected = dot(inputs_ref[...], weights_ref[...])
    gate_pre = projected[:, :hidden]
    up_pre = projected[:, hidden:]
    sigmoid_gate = jax.nn.sigmoid(gate_pre)
    gate_grad = cotangent * up_pre * sigmoid_gate * (1.0 + gate_pre * (1.0 - sigmoid_gate))
    up_grad = cotangent * gate_pre * sigmoid_gate
    pre_ref[:, :hidden] = gate_grad.astype(BF16)
    pre_ref[:, hidden:] = up_grad.astype(BF16)
    pre_grad = pre_ref[...]
    for at, size in chunks(width, 512):
        grad = dot_nt(pre_grad, weights_ref[at : at + size, :]).astype(BF16)
        start = 0
        for piece in grads:
            end = start + piece.shape[0]
            piece[:, at : at + size] = grad[start:end]
            start = end
    me = lax.axis_index("group").astype(jnp.int32)
    part = width // groups
    for k in range(groups):
        columns = pl.ds(pl.multiple_of((me ^ k) * part, part), part)
        term = dot_t(inputs_ref[:, columns], pre_grad)
        if k % 2:
            send_a[k // 2] = term[:, :hidden].astype(BF16)
        else:
            keep_a[k // 2] = term[:, :hidden]
        if k >= groups // 2:
            send_b[k - groups // 2] = term[:, hidden:].astype(BF16)
        else:
            keep_b[k] = term[:, hidden:]


def combine_kernel(select_ref, *refs):
    *pieces, out_ref, stacked_ref = refs
    start = 0
    for piece in pieces:
        end = start + piece.shape[0]
        stacked_ref[start:end, :] = piece[...]
        start = end
    select = select_ref[...]
    for at, size in chunks(out_ref.shape[1], 512):
        out_ref[:, at : at + size] = dot_t(select, stacked_ref[:, at : at + size]).astype(BF16)


def call(kernel, out_shapes, scratch, cost, *args, vmem=24 << 20):
    return pl.pallas_call(
        kernel,
        out_shape=out_shapes,
        in_specs=[VMEM] * len(args),
        out_specs=jax.tree.map(lambda _: VMEM, out_shapes),
        scratch_shapes=scratch,
        compiler_params=pltpu.CompilerParams(vmem_limit_bytes=vmem),
        cost_estimate=cost,
    )(*args)


def shape(dims, kind):
    return jax.ShapeDtypeStruct(dims, kind)


def exchange(pieces, experts, capacity):
    if len(pieces) == 1:
        block = pieces[0].reshape(experts, capacity, -1)
        moved = lax.all_to_all(block, "expert", split_axis=0, concat_axis=0, tiled=True)
        return [moved.reshape(experts * capacity, -1)]
    moved = list(pieces)
    half = experts // 2
    for k in list(range(half, experts)) + list(range(1, half)):
        pairs = [(e, e ^ k) for e in range(experts)]
        moved[k] = lax.ppermute(pieces[k], "expert", pairs)
    return moved


def sum_over_groups(send_a, keep_a, send_b, keep_b, groups):
    bits = groups.bit_length() - 1

    def flip(value, bit):
        return lax.ppermute(value, "group", [(g, g ^ (1 << bit)) for g in range(groups)])

    for step in range(bits):
        got_a = flip(send_a, step).astype(F32)
        got_b = flip(send_b, bits - 1 - step).astype(F32)
        if step == bits - 1:
            return jnp.concatenate([keep_a[0] + got_a[0], keep_b[0] + got_b[0]], axis=1)
        half = keep_a.shape[0] // 2
        send_a = (keep_a[1::2] + got_a[1::2]).astype(BF16)
        keep_a = keep_a[0::2] + got_a[0::2]
        send_b = (keep_b[half:] + got_b[half:]).astype(BF16)
        keep_b = keep_b[:half] + got_b[:half]


def on_device(tokens_in, hidden_grad, routing, gate_up):
    experts = lax.axis_size("expert")
    groups = lax.axis_size("group")
    rows = routing.shape[0]
    capacity = 2 * rows // experts
    slots = experts * capacity
    width = tokens_in.shape[1]
    hidden = hidden_grad.shape[1]
    joined = width + hidden
    weights = gate_up[0]
    direct = capacity % 16 == 0
    piece_rows = [capacity] * experts if direct else [slots]

    select, *pieces = call(
        functools.partial(dispatch_kernel, experts, direct),
        [shape((slots, rows), BF16)] + [shape((n, joined), BF16) for n in piece_rows],
        [],
        pl.CostEstimate(
            flops=2 * slots * rows * joined, bytes_accessed=2 * slots * joined, transcendentals=0
        ),
        routing.reshape(1, rows),
        tokens_in,
        hidden_grad,
    )
    arrived = exchange(pieces, experts, capacity)
    part = width // groups
    half = groups // 2
    count = len(piece_rows)
    block = (half, part, hidden)
    out = call(
        functools.partial(expert_kernel, groups, count),
        [shape((n, width), BF16) for n in piece_rows]
        + [shape(block, BF16), shape(block, F32), shape(block, BF16), shape(block, F32)],
        [pltpu.VMEM((slots, width), BF16), pltpu.VMEM((slots, 2 * hidden), BF16)],
        pl.CostEstimate(
            flops=6 * slots * width * 2 * hidden,
            bytes_accessed=4 * slots * joined + 4 * width * hidden,
            transcendentals=slots * hidden,
        ),
        *arrived,
        weights,
        vmem=32 << 20,
    )
    grads, sums = out[:count], out[count:]
    returned = exchange(grads, experts, capacity)
    weight_grad = sum_over_groups(*sums, groups)
    tokens_grad = call(
        combine_kernel,
        shape((rows, width), BF16),
        [pltpu.VMEM((slots, width), BF16)],
        pl.CostEstimate(
            flops=2 * slots * rows * width, bytes_accessed=2 * slots * width, transcendentals=0
        ),
        select,
        *returned,
    )
    return (tokens_grad, weight_grad[None])


def solution(mesh):
    return jax.shard_map(
        on_device,
        mesh=mesh,
        in_specs=(
            P(("expert", "group"), None),
            P(("expert", "group"), None),
            P(("expert", "group")),
            P("expert", None, None),
        ),
        out_specs=(P(("expert", "group"), None), P("expert", "group", None)),
        check_vma=False,
    )
```

```python
import functools

import jax
import jax.numpy as jnp
from jax import lax
from jax.experimental import pallas as pl
from jax.experimental.pallas import tpu as pltpu
from jax.sharding import PartitionSpec as P


BF16 = jnp.bfloat16
F32 = jnp.float32
VMEM = pl.BlockSpec(memory_space=pltpu.VMEM)
HBM = pl.BlockSpec(memory_space=pltpu.HBM)


def chunks(total, width):
    return [(at, min(width, total - at)) for at in range(0, total, width)]


def dot(a, b):
    return jnp.dot(a, b, preferred_element_type=F32)


def dot_t(a, b):
    return lax.dot_general(a, b, (((0,), (0,)), ((), ())), preferred_element_type=F32)


def dot_nt(a, b):
    return lax.dot_general(a, b, (((1,), (1,)), ((), ())), preferred_element_type=F32)


def stack(pieces, columns=slice(None)):
    if all(piece.shape[0] % 16 == 0 for piece in pieces):
        return jnp.concatenate([piece[:, columns] for piece in pieces], axis=0)
    return jnp.concatenate([piece[:, columns].astype(F32) for piece in pieces], axis=0).astype(BF16)


def unstack(value, pieces, columns):
    start = 0
    for piece in pieces:
        end = start + piece.shape[0]
        piece[:, columns] = value[start:end].astype(BF16)
        start = end


def ranks_of(block, experts):
    rows = block.shape[1]
    one_hot = block == lax.broadcasted_iota(jnp.int32, (experts, rows), 0)
    ones = jnp.where(one_hot, 1.0, 0.0)
    counts = dot(ones.astype(BF16), earlier(rows))
    return jnp.sum(counts * ones, axis=0, keepdims=True).astype(jnp.int32)


def earlier(rows):
    mask = lax.broadcasted_iota(jnp.int32, (rows, rows), 0) < lax.broadcasted_iota(
        jnp.int32, (rows, rows), 1
    )
    return jnp.where(mask, 1.0, 0.0).astype(BF16)


def one_hot_rows(target, count):
    return jnp.where(
        target == lax.broadcasted_iota(jnp.int32, (count, target.shape[1]), 0), 1.0, 0.0
    ).astype(BF16)


def load_inputs(routing_hbm, tokens_hbm, hidden_hbm, routing_ref, joined_ref, sems):
    width = tokens_hbm.shape[1]
    copies = [
        pltpu.make_async_copy(routing_hbm, routing_ref, sems.at[0]),
        pltpu.make_async_copy(tokens_hbm, joined_ref.at[:, :width], sems.at[1]),
        pltpu.make_async_copy(hidden_hbm, joined_ref.at[:, width:], sems.at[2]),
    ]
    for copy in copies:
        copy.start()
    return copies


def dispatch_kernel(experts, *refs):
    routing_hbm, tokens_hbm, hidden_hbm, select_ref, spill_ref, own_ref, *rest = refs
    near, low = rest[: experts // 2], rest[experts // 2 : experts]
    routing_ref, joined_ref, sems = rest[experts:]
    copies = load_inputs(routing_hbm, tokens_hbm, hidden_hbm, routing_ref, joined_ref, sems)
    rows, joined = joined_ref.shape
    half = experts // 2
    full, low_rows, up_rows = near[0].shape[0], low[0].shape[0], own_ref.shape[0] // half
    low_at = half * full
    own_at = low_at + half * low_rows
    spill_at = own_at + half * up_rows
    kept = low_rows + up_rows
    me = lax.axis_index("expert").astype(jnp.int32)
    copies[0].wait()
    block = routing_ref[...] ^ me
    rank = ranks_of(block, experts)
    far = block - half
    spilled = (far >= 0) & (rank >= kept)
    spilled_ones = jnp.broadcast_to(jnp.where(spilled, 1.0, 0.0), (8, rows)).astype(BF16)
    place = dot(spilled_ones, earlier(rows))[:1].astype(jnp.int32)
    target = jnp.where(
        far < 0,
        block * full + rank,
        jnp.where(
            rank < low_rows,
            low_at + far * low_rows + rank,
            jnp.where(
                spilled, spill_at + place, own_at + far * up_rows + (rank - low_rows)
            ),
        ),
    )
    select = one_hot_rows(target, select_ref.shape[0])
    select_ref[...] = select
    landing = jnp.where(spilled, far * up_rows + (up_rows - 1) - (rank - kept), -1)
    spill_ref[:, joined:] = dot_nt(
        select[spill_at:], one_hot_rows(landing, spill_ref.shape[1] - joined)
    ).astype(BF16)
    copies[1].wait()
    copies[2].wait()
    for at, size in chunks(joined, 256):
        columns = slice(at, at + size)
        placed = dot(select, joined_ref[:, columns])
        unstack(placed, [*near, *low, own_ref, spill_ref], columns)


def merge_kernel(own_ref, spill_ref, *piece_refs):
    slots, joined = own_ref.shape
    landing = spill_ref[:, joined:]
    for at, size in chunks(joined, 256):
        columns = slice(at, at + size)
        landed = dot_t(landing, spill_ref[:, columns])[:slots]
        unstack(landed + own_ref[:, columns].astype(F32), piece_refs, columns)


def split_kernel(spill_ref, *refs):
    *pieces, out_ref = refs
    slots = sum(piece.shape[0] for piece in pieces)
    joined = spill_ref.shape[1] - 128
    landing = spill_ref[:, joined:]
    for at, size in chunks(out_ref.shape[1], 512):
        columns = slice(at, at + size)
        value = stack(pieces, columns)
        pad = jnp.zeros((landing.shape[1] - slots, size), BF16)
        out_ref[:, columns] = dot(landing, jnp.concatenate([value, pad], axis=0)).astype(BF16)


def hidden_grads(inputs, cotangent, weights_ref):
    projected = dot(inputs, weights_ref[...])
    hidden = projected.shape[1] // 2
    gate_pre = projected[:, :hidden]
    up_pre = projected[:, hidden:]
    sigmoid_gate = jax.nn.sigmoid(gate_pre)
    gate_grad = cotangent * up_pre * sigmoid_gate * (1.0 + gate_pre * (1.0 - sigmoid_gate))
    up_grad = cotangent * gate_pre * sigmoid_gate
    return jnp.concatenate([gate_grad.astype(BF16), up_grad.astype(BF16)], axis=1)


def input_grads(pre_grad, weights_ref, pieces):
    for at, size in chunks(weights_ref.shape[0], 512):
        columns = slice(at, at + size)
        unstack(dot_nt(pre_grad, weights_ref[columns, :]), pieces, columns)


def near_kernel(count, *refs):
    pieces, (weights_ref, pre_ref), grads = refs[:count], refs[count : count + 2], refs[count + 2 :]
    width = weights_ref.shape[0]
    inputs = stack(pieces, slice(0, width))
    cotangent = stack(pieces, slice(width, None)).astype(F32)
    pre_ref[...] = hidden_grads(inputs, cotangent, weights_ref)
    input_grads(pre_ref[...], weights_ref, grads)


def far_kernel(groups, near_count, count, *refs):
    near = refs[:near_count]
    pieces = refs[near_count : near_count + count]
    near_pre_ref, weights_ref = refs[near_count + count : near_count + count + 2]
    rest = refs[near_count + count + 2 :]
    grads = rest[:count]
    send_a, keep_a, send_b, keep_b, inputs_ref, pre_ref = rest[count:]
    width, _ = weights_ref.shape
    split = near_pre_ref.shape[0]
    inputs_ref[:split, :] = stack(near, slice(0, width))
    pre_ref[:split, :] = near_pre_ref[...]
    low, up = pieces[: count // 2], pieces[count // 2 :]
    inputs = jnp.concatenate([stack(low, slice(0, width)), stack(up, slice(0, width))], axis=0)
    inputs_ref[split:, :] = inputs
    cotangent = jnp.concatenate(
        [stack(low, slice(width, None)), stack(up, slice(width, None))], axis=0
    ).astype(F32)
    pre_grad = hidden_grads(inputs_ref[split:, :], cotangent, weights_ref)
    pre_ref[split:, :] = pre_grad
    input_grads(pre_grad, weights_ref, grads)
    weight_terms(groups, inputs_ref, pre_ref, send_a, keep_a, send_b, keep_b)


def weight_terms(groups, inputs_ref, pre_ref, send_a, keep_a, send_b, keep_b):
    me = lax.axis_index("group").astype(jnp.int32)
    part = inputs_ref.shape[1] // groups
    hidden = pre_ref.shape[1] // 2
    pre_grad = pre_ref[...]
    for k in range(groups):
        columns = pl.ds(pl.multiple_of((me ^ k) * part, part), part)
        term = dot_t(inputs_ref[:, columns], pre_grad)
        if k % 2:
            send_a[k // 2] = term[:, :hidden].astype(BF16)
        else:
            keep_a[k // 2] = term[:, :hidden]
        if k >= groups // 2:
            send_b[k - groups // 2] = term[:, hidden:].astype(BF16)
        else:
            keep_b[k] = term[:, hidden:]


def combine_kernel(select_ref, *refs):
    *pieces, out_ref, stacked_ref = refs
    start = 0
    while pieces:
        rows = pieces[0].shape[0]
        run = pieces[: next((i for i, p in enumerate(pieces) if p.shape[0] != rows), len(pieces))]
        end = start + rows * len(run)
        stacked_ref[start:end, :] = stack(run)
        start, pieces = end, pieces[len(run) :]
    select = select_ref[...]
    for at, size in chunks(out_ref.shape[1], 512):
        out_ref[:, at : at + size] = dot_t(select, stacked_ref[:, at : at + size]).astype(BF16)


def call(kernel, out_shapes, scratch, flops, moved, args, specs=None, vmem=24 << 20):
    return pl.pallas_call(
        kernel,
        out_shape=out_shapes,
        in_specs=specs or [VMEM] * len(args),
        out_specs=jax.tree.map(lambda _: VMEM, out_shapes),
        scratch_shapes=scratch,
        compiler_params=pltpu.CompilerParams(vmem_limit_bytes=vmem),
        cost_estimate=pl.CostEstimate(flops=flops, bytes_accessed=moved, transcendentals=0),
    )(*args)


def shape(dims, kind=BF16):
    return jax.ShapeDtypeStruct(dims, kind)


def flip(value, axis, mask):
    size = lax.axis_size(axis)
    return lax.ppermute(value, axis, [(i, i ^ mask) for i in range(size)])


def sum_over_groups(send_a, keep_a, send_b, keep_b, groups):
    bits = groups.bit_length() - 1
    for step in range(bits):
        got_a = flip(send_a, "group", 1 << step).astype(F32)
        got_b = flip(send_b, "group", 1 << (bits - 1 - step)).astype(F32)
        if step == bits - 1:
            return jnp.concatenate([keep_a[0] + got_a[0], keep_b[0] + got_b[0]], axis=1)
        half = keep_a.shape[0] // 2
        send_a = (keep_a[1::2] + got_a[1::2]).astype(BF16)
        keep_a = keep_a[0::2] + got_a[0::2]
        send_b = (keep_b[half:] + got_b[half:]).astype(BF16)
        keep_b = keep_b[:half] + got_b[:half]


def term_shapes(groups, width, hidden):
    block = (groups // 2, width // groups, hidden)
    return [shape(block), shape(block, F32), shape(block), shape(block, F32)]


def paired(tokens_in, hidden_grad, routing, weights):
    experts = lax.axis_size("expert")
    groups = lax.axis_size("group")
    rows, width = tokens_in.shape
    hidden = hidden_grad.shape[1]
    joined = width + hidden
    half = experts // 2
    full, low_rows, up_rows = 2 * rows // experts, rows // experts, rows // (2 * experts)
    spill = rows // 4
    slots = half * (full + low_rows + up_rows) + spill
    lane = 128

    select, spilled, own, *pieces = call(
        functools.partial(dispatch_kernel, experts),
        [shape((slots, rows)), shape((spill, joined + lane)), shape((half * up_rows, joined))]
        + [shape((full, joined))] * half
        + [shape((low_rows, joined))] * half,
        [
            pltpu.VMEM((1, rows), jnp.int32),
            pltpu.VMEM((rows, joined), BF16),
            pltpu.SemaphoreType.DMA((3,)),
        ],
        2 * slots * rows * joined,
        2 * slots * joined,
        (routing.reshape(1, rows), tokens_in, hidden_grad),
        specs=[HBM] * 3,
        vmem=40 << 20,
    )
    near, low = pieces[:half], pieces[half:]
    landed = flip(spilled, "group", groups // 2)
    low = [flip(low[k], "expert", half + k) for k in range(half)]
    near = [near[0]] + [flip(near[k], "expert", k) for k in range(1, half)]
    up = call(
        merge_kernel,
        [shape((up_rows, joined))] * half,
        [],
        2 * spill * lane * joined,
        4 * half * up_rows * joined,
        (own, landed),
    )
    up = [flip(up[k], "expert", half + k) for k in range(half)]

    near_slots, far_slots = half * full, half * (low_rows + up_rows)
    near_pre, *near_grads = call(
        functools.partial(near_kernel, half),
        [shape((near_slots, 2 * hidden))] + [shape((full, width))] * half,
        [],
        8 * near_slots * width * hidden,
        4 * near_slots * joined,
        (*near, weights),
    )
    out = call(
        functools.partial(far_kernel, groups, half, 2 * half),
        [shape((low_rows, width))] * half
        + [shape((up_rows, width))] * half
        + term_shapes(groups, width, hidden),
        [
            pltpu.VMEM((near_slots + far_slots, width), BF16),
            pltpu.VMEM((near_slots + far_slots, 2 * hidden), BF16),
        ],
        12 * (near_slots + far_slots) * width * hidden,
        4 * (near_slots + far_slots) * joined,
        (*near, *low, *up, near_pre, weights),
        vmem=32 << 20,
    )
    low_grads, up_grads, terms = out[:half], out[half : 2 * half], out[2 * half :]
    near_grads = [near_grads[0]] + [flip(near_grads[k], "expert", k) for k in range(1, half)]
    up_grads = [flip(up_grads[k], "expert", half + k) for k in range(half)]
    low_grads = [flip(low_grads[k], "expert", half + k) for k in range(half)]
    spilled_grad = call(
        split_kernel,
        shape((spill, width)),
        [],
        2 * spill * lane * width,
        4 * half * up_rows * width,
        (landed, *up_grads),
    )
    spilled_grad = flip(spilled_grad, "group", groups // 2)
    weight_grad = sum_over_groups(*terms, groups)
    tokens_grad = call(
        combine_kernel,
        shape((rows, width)),
        [pltpu.VMEM((slots, width), BF16)],
        2 * slots * rows * width,
        2 * slots * width,
        (select, *near_grads, *low_grads, *up_grads, spilled_grad),
    )
    return tokens_grad, weight_grad


def whole_dispatch_kernel(experts, routing_hbm, tokens_hbm, hidden_hbm, select_ref, out_ref, *rest):
    routing_ref, joined_ref, sems = rest
    copies = load_inputs(routing_hbm, tokens_hbm, hidden_hbm, routing_ref, joined_ref, sems)
    copies[0].wait()
    block = routing_ref[...]
    slots = select_ref.shape[0]
    select = one_hot_rows(block * (slots // experts) + ranks_of(block, experts), slots)
    select_ref[...] = select
    copies[1].wait()
    copies[2].wait()
    for at, size in chunks(out_ref.shape[1], 256):
        columns = slice(at, at + size)
        out_ref[:, columns] = dot(select, joined_ref[:, columns]).astype(BF16)


def whole_expert_kernel(groups, rows_ref, weights_ref, grad_ref, *refs):
    *terms, inputs_ref, pre_ref = refs
    width = weights_ref.shape[0]
    inputs_ref[...] = rows_ref[:, :width]
    pre_ref[...] = hidden_grads(inputs_ref[...], rows_ref[:, width:].astype(F32), weights_ref)
    input_grads(pre_ref[...], weights_ref, [grad_ref])
    weight_terms(groups, inputs_ref, pre_ref, *terms)


def unpaired(tokens_in, hidden_grad, routing, weights):
    experts = lax.axis_size("expert")
    groups = lax.axis_size("group")
    rows, width = tokens_in.shape
    hidden = hidden_grad.shape[1]
    joined = width + hidden
    capacity = 2 * rows // experts
    slots = experts * capacity

    def exchange(value):
        block = value.reshape(experts, capacity, -1)
        moved = lax.all_to_all(block, "expert", split_axis=0, concat_axis=0, tiled=True)
        return moved.reshape(slots, -1)

    select, outgoing = call(
        functools.partial(whole_dispatch_kernel, experts),
        [shape((slots, rows)), shape((slots, joined))],
        [
            pltpu.VMEM((1, rows), jnp.int32),
            pltpu.VMEM((rows, joined), BF16),
            pltpu.SemaphoreType.DMA((3,)),
        ],
        2 * slots * rows * joined,
        2 * slots * joined,
        (routing.reshape(1, rows), tokens_in, hidden_grad),
        specs=[HBM] * 3,
    )
    grad, *terms = call(
        functools.partial(whole_expert_kernel, groups),
        [shape((slots, width))] + term_shapes(groups, width, hidden),
        [pltpu.VMEM((slots, width), BF16), pltpu.VMEM((slots, 2 * hidden), BF16)],
        12 * slots * width * hidden,
        4 * slots * joined,
        (exchange(outgoing), weights),
        vmem=32 << 20,
    )
    weight_grad = sum_over_groups(*terms, groups)
    tokens_grad = call(
        combine_kernel,
        shape((rows, width)),
        [pltpu.VMEM((slots, width), BF16)],
        2 * slots * rows * width,
        2 * slots * width,
        (select, exchange(grad)),
    )
    return tokens_grad, weight_grad


def can_pair(mesh, rows):
    experts, groups = mesh.shape["expert"], mesh.shape["group"]
    return groups % 2 == 0 and rows % (16 * experts) == 0 and experts <= 16


def on_device(pair, tokens_in, hidden_grad, routing, gate_up):
    run = paired if pair else unpaired
    tokens_grad, weight_grad = run(tokens_in, hidden_grad, routing, gate_up[0])
    return (tokens_grad, weight_grad[None])


def solution(mesh):
    devices = mesh.shape["expert"] * mesh.shape["group"]

    def whole(tokens_in, hidden_grad, routing, gate_up):
        pair = can_pair(mesh, routing.shape[0] // devices)
        return jax.shard_map(
            functools.partial(on_device, pair),
            mesh=mesh,
            in_specs=(
                P(("expert", "group"), None),
                P(("expert", "group"), None),
                P(("expert", "group")),
                P("expert", None, None),
            ),
            out_specs=(P(("expert", "group"), None), P("expert", "group", None)),
            check_vma=False,
        )(tokens_in, hidden_grad, routing, gate_up)

    return whole
```

```python
import functools

import jax
import jax.numpy as jnp
from jax import lax
from jax.experimental import pallas as pl
from jax.experimental.pallas import tpu as pltpu
from jax.sharding import PartitionSpec as P


BF16 = jnp.bfloat16
F32 = jnp.float32
VMEM = pl.BlockSpec(memory_space=pltpu.VMEM)
HBM = pl.BlockSpec(memory_space=pltpu.HBM)


def chunks(total, width):
    return [(at, min(width, total - at)) for at in range(0, total, width)]


def dot(a, b):
    return jnp.dot(a, b, preferred_element_type=F32)


def dot_t(a, b):
    return lax.dot_general(a, b, (((0,), (0,)), ((), ())), preferred_element_type=F32)


def dot_nt(a, b):
    return lax.dot_general(a, b, (((1,), (1,)), ((), ())), preferred_element_type=F32)


def stack(pieces, columns=slice(None)):
    if all(piece.shape[0] % 16 == 0 for piece in pieces):
        return jnp.concatenate([piece[:, columns] for piece in pieces], axis=0)
    return jnp.concatenate([piece[:, columns].astype(F32) for piece in pieces], axis=0).astype(BF16)


def unstack(value, pieces, columns):
    start = 0
    for piece in pieces:
        end = start + piece.shape[0]
        piece[:, columns] = value[start:end].astype(BF16)
        start = end


def ranks_of(block, experts):
    rows = block.shape[1]
    one_hot = block == lax.broadcasted_iota(jnp.int32, (experts, rows), 0)
    ones = jnp.where(one_hot, 1.0, 0.0)
    counts = dot(ones.astype(BF16), earlier(rows))
    return jnp.sum(counts * ones, axis=0, keepdims=True).astype(jnp.int32)


def earlier(rows):
    mask = lax.broadcasted_iota(jnp.int32, (rows, rows), 0) < lax.broadcasted_iota(
        jnp.int32, (rows, rows), 1
    )
    return jnp.where(mask, 1.0, 0.0).astype(BF16)


def one_hot_rows(target, count):
    return jnp.where(
        target == lax.broadcasted_iota(jnp.int32, (count, target.shape[1]), 0), 1.0, 0.0
    ).astype(BF16)


def load_inputs(routing_hbm, tokens_hbm, hidden_hbm, routing_ref, joined_ref, sems):
    width = tokens_hbm.shape[1]
    copies = [
        pltpu.make_async_copy(routing_hbm, routing_ref, sems.at[0]),
        pltpu.make_async_copy(tokens_hbm, joined_ref.at[:, :width], sems.at[1]),
        pltpu.make_async_copy(hidden_hbm, joined_ref.at[:, width:], sems.at[2]),
    ]
    for copy in copies:
        copy.start()
    return copies


def dispatch_kernel(experts, *refs):
    routing_hbm, tokens_hbm, hidden_hbm, select_ref, spill_ref, own_ref, *rest = refs
    near, low = rest[: experts // 2], rest[experts // 2 : experts]
    routing_ref, joined_ref, sems = rest[experts:]
    copies = load_inputs(routing_hbm, tokens_hbm, hidden_hbm, routing_ref, joined_ref, sems)
    rows, joined = joined_ref.shape
    half = experts // 2
    full, low_rows, up_rows = near[0].shape[0], low[0].shape[0], own_ref.shape[0] // half
    low_at = half * full
    own_at = low_at + half * low_rows
    spill_at = own_at + half * up_rows
    kept = low_rows + up_rows
    me = lax.axis_index("expert").astype(jnp.int32)
    copies[0].wait()
    block = routing_ref[...] ^ me
    rank = ranks_of(block, experts)
    far = block - half
    spilled = (far >= 0) & (rank >= kept)
    spilled_ones = jnp.broadcast_to(jnp.where(spilled, 1.0, 0.0), (8, rows)).astype(BF16)
    place = dot(spilled_ones, earlier(rows))[:1].astype(jnp.int32)
    target = jnp.where(
        far < 0,
        block * full + rank,
        jnp.where(
            rank < low_rows,
            low_at + far * low_rows + rank,
            jnp.where(
                spilled, spill_at + place, own_at + far * up_rows + (rank - low_rows)
            ),
        ),
    )
    select = one_hot_rows(target, select_ref.shape[0])
    select_ref[...] = select
    landing = jnp.where(spilled, far * up_rows + (up_rows - 1) - (rank - kept), -1)
    spill_ref[:, joined:] = dot_nt(
        select[spill_at:], one_hot_rows(landing, spill_ref.shape[1] - joined)
    ).astype(BF16)
    copies[1].wait()
    copies[2].wait()
    for at, size in chunks(joined, 256):
        columns = slice(at, at + size)
        placed = dot(select, joined_ref[:, columns])
        unstack(placed, [*near, *low, own_ref, spill_ref], columns)


def merge_kernel(own_ref, spill_ref, *piece_refs):
    slots, joined = own_ref.shape
    landing = spill_ref[:, joined:]
    for at, size in chunks(joined, 256):
        columns = slice(at, at + size)
        landed = dot_t(landing, spill_ref[:, columns])[:slots]
        unstack(landed + own_ref[:, columns].astype(F32), piece_refs, columns)


def split_kernel(spill_ref, *refs):
    *pieces, out_ref = refs
    slots = sum(piece.shape[0] for piece in pieces)
    joined = spill_ref.shape[1] - 128
    landing = spill_ref[:, joined:]
    for at, size in chunks(out_ref.shape[1], 512):
        columns = slice(at, at + size)
        value = stack(pieces, columns)
        pad = jnp.zeros((landing.shape[1] - slots, size), BF16)
        out_ref[:, columns] = dot(landing, jnp.concatenate([value, pad], axis=0)).astype(BF16)


def hidden_grads(inputs, cotangent, weights_ref):
    projected = dot(inputs, weights_ref[...])
    hidden = projected.shape[1] // 2
    gate_pre = projected[:, :hidden]
    up_pre = projected[:, hidden:]
    sigmoid_gate = jax.nn.sigmoid(gate_pre)
    gate_grad = cotangent * up_pre * sigmoid_gate * (1.0 + gate_pre * (1.0 - sigmoid_gate))
    up_grad = cotangent * gate_pre * sigmoid_gate
    return jnp.concatenate([gate_grad.astype(BF16), up_grad.astype(BF16)], axis=1)


def input_grads(pre_grad, weights_ref, pieces):
    for at, size in chunks(weights_ref.shape[0], 512):
        columns = slice(at, at + size)
        unstack(dot_nt(pre_grad, weights_ref[columns, :]), pieces, columns)


def load_kernel(source, target, sem):
    copy = pltpu.make_async_copy(source, target, sem)
    copy.start()
    copy.wait()


def near_kernel(count, *refs):
    pieces, (weights_ref, pre_ref), grads = refs[:count], refs[count : count + 2], refs[count + 2 :]
    width = weights_ref.shape[0]
    inputs = stack(pieces, slice(0, width))
    cotangent = stack(pieces, slice(width, None)).astype(F32)
    pre_ref[...] = hidden_grads(inputs, cotangent, weights_ref)
    input_grads(pre_ref[...], weights_ref, grads)


def far_kernel(groups, near_count, count, *refs):
    near = refs[:near_count]
    pieces = refs[near_count : near_count + count]
    near_pre_ref, weights_ref = refs[near_count + count : near_count + count + 2]
    rest = refs[near_count + count + 2 :]
    grads = rest[:count]
    send_a, keep_a, send_b, keep_b, inputs_ref, pre_ref = rest[count:]
    width, _ = weights_ref.shape
    split = near_pre_ref.shape[0]
    inputs_ref[:split, :] = stack(near, slice(0, width))
    pre_ref[:split, :] = near_pre_ref[...]
    low, up = pieces[: count // 2], pieces[count // 2 :]
    inputs = jnp.concatenate([stack(low, slice(0, width)), stack(up, slice(0, width))], axis=0)
    inputs_ref[split:, :] = inputs
    cotangent = jnp.concatenate(
        [stack(low, slice(width, None)), stack(up, slice(width, None))], axis=0
    ).astype(F32)
    pre_grad = hidden_grads(inputs_ref[split:, :], cotangent, weights_ref)
    pre_ref[split:, :] = pre_grad
    input_grads(pre_grad, weights_ref, grads)
    weight_terms(groups, inputs_ref, pre_ref, send_a, keep_a, send_b, keep_b)


def weight_terms(groups, inputs_ref, pre_ref, send_a, keep_a, send_b, keep_b):
    me = lax.axis_index("group").astype(jnp.int32)
    part = inputs_ref.shape[1] // groups
    hidden = pre_ref.shape[1] // 2
    pre_grad = pre_ref[...]
    for k in range(groups):
        columns = pl.ds(pl.multiple_of((me ^ k) * part, part), part)
        term = dot_t(inputs_ref[:, columns], pre_grad)
        if k % 2:
            send_a[k // 2] = term[:, :hidden].astype(BF16)
        else:
            keep_a[k // 2] = term[:, :hidden]
        if k >= groups // 2:
            send_b[k - groups // 2] = term[:, hidden:].astype(BF16)
        else:
            keep_b[k] = term[:, hidden:]


def combine_kernel(select_ref, *refs):
    *pieces, out_ref, stacked_ref = refs
    start = 0
    while pieces:
        rows = pieces[0].shape[0]
        run = pieces[: next((i for i, p in enumerate(pieces) if p.shape[0] != rows), len(pieces))]
        end = start + rows * len(run)
        stacked_ref[start:end, :] = stack(run)
        start, pieces = end, pieces[len(run) :]
    select = select_ref[...]
    for at, size in chunks(out_ref.shape[1], 512):
        out_ref[:, at : at + size] = dot_t(select, stacked_ref[:, at : at + size]).astype(BF16)


def call(kernel, out_shapes, scratch, flops, moved, args, specs=None, vmem=24 << 20):
    if specs is not None:
        args = [
            pltpu.with_memory_space_constraint(arg, pltpu.HBM) if spec is HBM else arg
            for arg, spec in zip(args, specs)
        ]
    return pl.pallas_call(
        kernel,
        out_shape=out_shapes,
        in_specs=specs or [VMEM] * len(args),
        out_specs=jax.tree.map(lambda _: VMEM, out_shapes),
        scratch_shapes=scratch,
        compiler_params=pltpu.CompilerParams(vmem_limit_bytes=vmem),
        cost_estimate=pl.CostEstimate(flops=flops, bytes_accessed=moved, transcendentals=0),
    )(*args)


def shape(dims, kind=BF16):
    return jax.ShapeDtypeStruct(dims, kind)


def flip(value, axis, mask):
    size = lax.axis_size(axis)
    return lax.ppermute(value, axis, [(i, i ^ mask) for i in range(size)])


def sum_over_groups(send_a, keep_a, send_b, keep_b, groups):
    bits = groups.bit_length() - 1
    for step in range(bits):
        got_a = flip(send_a, "group", 1 << step).astype(F32)
        got_b = flip(send_b, "group", 1 << (bits - 1 - step)).astype(F32)
        if step == bits - 1:
            return jnp.concatenate([keep_a[0] + got_a[0], keep_b[0] + got_b[0]], axis=1)
        half = keep_a.shape[0] // 2
        send_a = (keep_a[1::2] + got_a[1::2]).astype(BF16)
        keep_a = keep_a[0::2] + got_a[0::2]
        send_b = (keep_b[half:] + got_b[half:]).astype(BF16)
        keep_b = keep_b[:half] + got_b[:half]


def term_shapes(groups, width, hidden):
    block = (groups // 2, width // groups, hidden)
    return [shape(block), shape(block, F32), shape(block), shape(block, F32)]


def paired(tokens_in, hidden_grad, routing, weights):
    experts = lax.axis_size("expert")
    groups = lax.axis_size("group")
    rows, width = tokens_in.shape
    hidden = hidden_grad.shape[1]
    joined = width + hidden
    half = experts // 2
    full, low_rows, up_rows = 2 * rows // experts, rows // experts, rows // (2 * experts)
    spill = rows // 4
    slots = half * (full + low_rows + up_rows) + spill
    lane = 128

    select, spilled, own, *pieces = call(
        functools.partial(dispatch_kernel, experts),
        [shape((slots, rows)), shape((spill, joined + lane)), shape((half * up_rows, joined))]
        + [shape((full, joined))] * half
        + [shape((low_rows, joined))] * half,
        [
            pltpu.VMEM((1, rows), jnp.int32),
            pltpu.VMEM((rows, joined), BF16),
            pltpu.SemaphoreType.DMA((3,)),
        ],
        2 * slots * rows * joined,
        2 * slots * joined,
        (routing.reshape(1, rows), tokens_in, hidden_grad),
        specs=[HBM] * 3,
    )
    near, low = pieces[:half], pieces[half:]
    landed = flip(spilled, "group", groups // 2)
    low = [flip(low[k], "expert", half + k) for k in range(half)]
    near = [near[0]] + [flip(near[k], "expert", k) for k in range(1, half)]
    up = call(
        merge_kernel,
        [shape((up_rows, joined))] * half,
        [],
        2 * spill * lane * joined,
        4 * half * up_rows * joined,
        (own, landed),
    )
    up = [flip(up[k], "expert", half + k) for k in range(half)]

    weights = call(
        load_kernel,
        shape(weights.shape),
        [pltpu.SemaphoreType.DMA],
        0,
        weights.size * 2,
        (weights,),
        specs=[HBM],
    )
    near_slots, far_slots = half * full, half * (low_rows + up_rows)
    near_pre, *near_grads = call(
        functools.partial(near_kernel, half),
        [shape((near_slots, 2 * hidden))] + [shape((full, width))] * half,
        [],
        8 * near_slots * width * hidden,
        4 * near_slots * joined,
        (*near, weights),
    )
    out = call(
        functools.partial(far_kernel, groups, half, 2 * half),
        [shape((low_rows, width))] * half
        + [shape((up_rows, width))] * half
        + term_shapes(groups, width, hidden),
        [
            pltpu.VMEM((near_slots + far_slots, width), BF16),
            pltpu.VMEM((near_slots + far_slots, 2 * hidden), BF16),
        ],
        12 * (near_slots + far_slots) * width * hidden,
        4 * (near_slots + far_slots) * joined,
        (*near, *low, *up, near_pre, weights),
        vmem=32 << 20,
    )
    low_grads, up_grads, terms = out[:half], out[half : 2 * half], out[2 * half :]
    near_grads = [near_grads[0]] + [flip(near_grads[k], "expert", k) for k in range(1, half)]
    up_grads = [flip(up_grads[k], "expert", half + k) for k in range(half)]
    low_grads = [flip(low_grads[k], "expert", half + k) for k in range(half)]
    spilled_grad = call(
        split_kernel,
        shape((spill, width)),
        [],
        2 * spill * lane * width,
        4 * half * up_rows * width,
        (landed, *up_grads),
    )
    spilled_grad = flip(spilled_grad, "group", groups // 2)
    weight_grad = sum_over_groups(*terms, groups)
    tokens_grad = call(
        combine_kernel,
        shape((rows, width)),
        [pltpu.VMEM((slots, width), BF16)],
        2 * slots * rows * width,
        2 * slots * width,
        (select, *near_grads, *low_grads, *up_grads, spilled_grad),
    )
    return tokens_grad, weight_grad


def whole_dispatch_kernel(experts, routing_hbm, tokens_hbm, hidden_hbm, select_ref, out_ref, *rest):
    routing_ref, joined_ref, sems = rest
    copies = load_inputs(routing_hbm, tokens_hbm, hidden_hbm, routing_ref, joined_ref, sems)
    copies[0].wait()
    block = routing_ref[...]
    slots = select_ref.shape[0]
    select = one_hot_rows(block * (slots // experts) + ranks_of(block, experts), slots)
    select_ref[...] = select
    copies[1].wait()
    copies[2].wait()
    for at, size in chunks(out_ref.shape[1], 256):
        columns = slice(at, at + size)
        out_ref[:, columns] = dot(select, joined_ref[:, columns]).astype(BF16)


def whole_expert_kernel(groups, rows_ref, weights_ref, grad_ref, *refs):
    *terms, inputs_ref, pre_ref = refs
    width = weights_ref.shape[0]
    inputs_ref[...] = rows_ref[:, :width]
    pre_ref[...] = hidden_grads(inputs_ref[...], rows_ref[:, width:].astype(F32), weights_ref)
    input_grads(pre_ref[...], weights_ref, [grad_ref])
    weight_terms(groups, inputs_ref, pre_ref, *terms)


def unpaired(tokens_in, hidden_grad, routing, weights):
    experts = lax.axis_size("expert")
    groups = lax.axis_size("group")
    rows, width = tokens_in.shape
    hidden = hidden_grad.shape[1]
    joined = width + hidden
    capacity = 2 * rows // experts
    slots = experts * capacity

    def exchange(value):
        block = value.reshape(experts, capacity, -1)
        moved = lax.all_to_all(block, "expert", split_axis=0, concat_axis=0, tiled=True)
        return moved.reshape(slots, -1)

    select, outgoing = call(
        functools.partial(whole_dispatch_kernel, experts),
        [shape((slots, rows)), shape((slots, joined))],
        [
            pltpu.VMEM((1, rows), jnp.int32),
            pltpu.VMEM((rows, joined), BF16),
            pltpu.SemaphoreType.DMA((3,)),
        ],
        2 * slots * rows * joined,
        2 * slots * joined,
        (routing.reshape(1, rows), tokens_in, hidden_grad),
        specs=[HBM] * 3,
    )
    grad, *terms = call(
        functools.partial(whole_expert_kernel, groups),
        [shape((slots, width))] + term_shapes(groups, width, hidden),
        [pltpu.VMEM((slots, width), BF16), pltpu.VMEM((slots, 2 * hidden), BF16)],
        12 * slots * width * hidden,
        4 * slots * joined,
        (exchange(outgoing), weights),
        vmem=32 << 20,
    )
    weight_grad = sum_over_groups(*terms, groups)
    tokens_grad = call(
        combine_kernel,
        shape((rows, width)),
        [pltpu.VMEM((slots, width), BF16)],
        2 * slots * rows * width,
        2 * slots * width,
        (select, exchange(grad)),
    )
    return tokens_grad, weight_grad


def can_pair(mesh, rows):
    experts, groups = mesh.shape["expert"], mesh.shape["group"]
    return groups % 2 == 0 and rows % (16 * experts) == 0 and experts <= 16


def on_device(pair, tokens_in, hidden_grad, routing, gate_up):
    run = paired if pair else unpaired
    tokens_grad, weight_grad = run(tokens_in, hidden_grad, routing, gate_up[0])
    return (tokens_grad, weight_grad[None])


def solution(mesh):
    devices = mesh.shape["expert"] * mesh.shape["group"]

    def whole(tokens_in, hidden_grad, routing, gate_up):
        pair = can_pair(mesh, routing.shape[0] // devices)
        return jax.shard_map(
            functools.partial(on_device, pair),
            mesh=mesh,
            in_specs=(
                P(("expert", "group"), None),
                P(("expert", "group"), None),
                P(("expert", "group")),
                P("expert", None, None),
            ),
            out_specs=(P(("expert", "group"), None), P("expert", "group", None)),
            check_vma=False,
        )(tokens_in, hidden_grad, routing, gate_up)

    return whole
```

```python
import functools

import jax
import jax.numpy as jnp
from jax import lax
from jax.experimental import pallas as pl
from jax.experimental.pallas import tpu as pltpu
from jax.sharding import PartitionSpec as P


BF16 = jnp.bfloat16
F32 = jnp.float32
LATE = ("up0", "up1", "up2", "up3")
PARTS = 1
VMEM = pl.BlockSpec(memory_space=pltpu.VMEM)
HBM = pl.BlockSpec(memory_space=pltpu.HBM)


def chunks(total, width):
    return [(at, min(width, total - at)) for at in range(0, total, width)]


def dot(a, b):
    return jnp.dot(a, b, preferred_element_type=F32)


def dot_t(a, b):
    return lax.dot_general(a, b, (((0,), (0,)), ((), ())), preferred_element_type=F32)


def dot_nt(a, b):
    return lax.dot_general(a, b, (((1,), (1,)), ((), ())), preferred_element_type=F32)


def stack(pieces, columns=slice(None)):
    if all(piece.shape[0] % 16 == 0 for piece in pieces):
        return jnp.concatenate([piece[:, columns] for piece in pieces], axis=0)
    return jnp.concatenate([piece[:, columns].astype(F32) for piece in pieces], axis=0).astype(BF16)


def unstack(value, pieces, columns):
    start = 0
    for piece in pieces:
        end = start + piece.shape[0]
        piece[:, columns] = value[start:end].astype(BF16)
        start = end


def ranks_of(block, experts):
    rows = block.shape[1]
    one_hot = block == lax.broadcasted_iota(jnp.int32, (experts, rows), 0)
    ones = jnp.where(one_hot, 1.0, 0.0)
    counts = dot(ones.astype(BF16), earlier(rows))
    return jnp.sum(counts * ones, axis=0, keepdims=True).astype(jnp.int32)


def earlier(rows):
    mask = lax.broadcasted_iota(jnp.int32, (rows, rows), 0) < lax.broadcasted_iota(
        jnp.int32, (rows, rows), 1
    )
    return jnp.where(mask, 1.0, 0.0).astype(BF16)


def one_hot_rows(target, count):
    return jnp.where(
        target == lax.broadcasted_iota(jnp.int32, (count, target.shape[1]), 0), 1.0, 0.0
    ).astype(BF16)


def load_inputs(routing_hbm, tokens_hbm, hidden_hbm, routing_ref, joined_ref, sems):
    width = tokens_hbm.shape[1]
    copies = [
        pltpu.make_async_copy(routing_hbm, routing_ref, sems.at[0]),
        pltpu.make_async_copy(tokens_hbm, joined_ref.at[:, :width], sems.at[1]),
        pltpu.make_async_copy(hidden_hbm, joined_ref.at[:, width:], sems.at[2]),
    ]
    for copy in copies:
        copy.start()
    return copies


def dispatch_kernel(experts, *refs):
    routing_hbm, tokens_hbm, hidden_hbm, select_ref, spill_ref, own_ref, *rest = refs
    near, low = rest[: experts // 2], rest[experts // 2 : experts]
    routing_ref, joined_ref, sems = rest[experts:]
    copies = load_inputs(routing_hbm, tokens_hbm, hidden_hbm, routing_ref, joined_ref, sems)
    rows, joined = joined_ref.shape
    half = experts // 2
    full, low_rows, up_rows = near[0].shape[0], low[0].shape[0], own_ref.shape[0] // half
    low_at = half * full
    own_at = low_at + half * low_rows
    spill_at = own_at + half * up_rows
    kept = low_rows + up_rows
    me = lax.axis_index("expert").astype(jnp.int32)
    copies[0].wait()
    block = routing_ref[...] ^ me
    rank = ranks_of(block, experts)
    far = block - half
    spilled = (far >= 0) & (rank >= kept)
    spilled_ones = jnp.broadcast_to(jnp.where(spilled, 1.0, 0.0), (8, rows)).astype(BF16)
    place = dot(spilled_ones, earlier(rows))[:1].astype(jnp.int32)
    target = jnp.where(
        far < 0,
        block * full + rank,
        jnp.where(
            rank < low_rows,
            low_at + far * low_rows + rank,
            jnp.where(
                spilled, spill_at + place, own_at + far * up_rows + (rank - low_rows)
            ),
        ),
    )
    select = one_hot_rows(target, select_ref.shape[0])
    select_ref[...] = select
    landing = jnp.where(spilled, far * up_rows + (up_rows - 1) - (rank - kept), -1)
    spill_ref[:, joined:] = dot_nt(
        select[spill_at:], one_hot_rows(landing, spill_ref.shape[1] - joined)
    ).astype(BF16)
    copies[1].wait()
    copies[2].wait()
    for at, size in chunks(joined, 256):
        columns = slice(at, at + size)
        placed = dot(select, joined_ref[:, columns])
        unstack(placed, [*near, *low, own_ref, spill_ref], columns)


def merge_kernel(own_ref, spill_ref, *piece_refs):
    slots, joined = own_ref.shape
    landing = spill_ref[:, joined:]
    for at, size in chunks(joined, 256):
        columns = slice(at, at + size)
        landed = dot_t(landing, spill_ref[:, columns])[:slots]
        unstack(landed + own_ref[:, columns].astype(F32), piece_refs, columns)


def split_kernel(spill_ref, *refs):
    *pieces, out_ref = refs
    slots = sum(piece.shape[0] for piece in pieces)
    joined = spill_ref.shape[1] - 128
    landing = spill_ref[:, joined:]
    for at, size in chunks(out_ref.shape[1], 512):
        columns = slice(at, at + size)
        value = stack(pieces, columns)
        pad = jnp.zeros((landing.shape[1] - slots, size), BF16)
        out_ref[:, columns] = dot(landing, jnp.concatenate([value, pad], axis=0)).astype(BF16)


def hidden_grads(inputs, cotangent, weights_ref):
    projected = dot(inputs, weights_ref[...])
    hidden = projected.shape[1] // 2
    gate_pre = projected[:, :hidden]
    up_pre = projected[:, hidden:]
    sigmoid_gate = jax.nn.sigmoid(gate_pre)
    gate_grad = cotangent * up_pre * sigmoid_gate * (1.0 + gate_pre * (1.0 - sigmoid_gate))
    up_grad = cotangent * gate_pre * sigmoid_gate
    return jnp.concatenate([gate_grad.astype(BF16), up_grad.astype(BF16)], axis=1)


def input_grads(pre_grad, weights_ref, pieces):
    for at, size in chunks(weights_ref.shape[0], 512):
        columns = slice(at, at + size)
        unstack(dot_nt(pre_grad, weights_ref[columns, :]), pieces, columns)


def load_kernel(source, target, sem):
    copy = pltpu.make_async_copy(source, target, sem)
    copy.start()
    copy.wait()


def rows_grads(pieces, weights_ref, inputs_ref, pre_ref, grads):
    width = weights_ref.shape[0]
    start = 0
    for run in runs(pieces):
        end = start + sum(piece.shape[0] for piece in run)
        inputs_ref[start:end, :] = stack(run, slice(0, width))
        start = end
    cotangent = jnp.concatenate(
        [stack(run, slice(width, None)).astype(F32) for run in runs(pieces)], axis=0
    )
    pre_ref[...] = hidden_grads(inputs_ref[...], cotangent, weights_ref)
    input_grads(pre_ref[...], weights_ref, grads)


def early_kernel(count, *refs):
    pieces, (weights_ref, inputs_ref, pre_ref), grads = (
        refs[:count],
        refs[count : count + 3],
        refs[count + 3 :],
    )
    rows_grads(pieces, weights_ref, inputs_ref, pre_ref, grads)


def late_kernel(groups, parts, count, *refs):
    early_inputs_ref, early_pre_ref, weights_ref = refs[:3]
    pieces, rest = refs[3 : count + 3], refs[count + 3 :]
    grads, terms, (inputs_ref, pre_ref) = rest[:count], rest[count:-2], rest[-2:]
    split = early_pre_ref.shape[0]
    inputs_ref[:split, :] = early_inputs_ref[...]
    pre_ref[:split, :] = early_pre_ref[...]
    rows_grads(pieces, weights_ref, inputs_ref.at[split:, :], pre_ref.at[split:, :], grads)
    weight_terms(groups, parts, inputs_ref, pre_ref, terms)


def weight_terms(groups, parts, inputs_ref, pre_ref, terms):
    me = lax.axis_index("group").astype(jnp.int32)
    part = inputs_ref.shape[1] // groups
    hidden = pre_ref.shape[1] // 2
    pre_grad = pre_ref[...]
    for k in range(groups):
        columns = pl.ds(pl.multiple_of((me ^ k) * part, part), part)
        term = dot_t(inputs_ref[:, columns], pre_grad)
        for chunk in range(parts):
            send_a, keep_a, send_b, keep_b = terms[4 * chunk : 4 * chunk + 4]
            size = part // parts
            rows = slice(chunk * size, (chunk + 1) * size)
            if k % 2:
                send_a[k // 2] = term[rows, :hidden].astype(BF16)
            else:
                keep_a[k // 2] = term[rows, :hidden]
            if k >= groups // 2:
                send_b[k - groups // 2] = term[rows, hidden:].astype(BF16)
            else:
                keep_b[k] = term[rows, hidden:]


def runs(pieces):
    found = []
    for piece in pieces:
        if found and found[-1][0].shape[0] == piece.shape[0]:
            found[-1].append(piece)
        else:
            found.append([piece])
    return found


def combine_kernel(select_ref, *refs):
    *pieces, out_ref, stacked_ref = refs
    start = 0
    for run in runs(pieces):
        end = start + sum(piece.shape[0] for piece in run)
        stacked_ref[start:end, :] = stack(run)
        start = end
    select = select_ref[...]
    for at, size in chunks(out_ref.shape[1], 512):
        out_ref[:, at : at + size] = dot_t(select, stacked_ref[:, at : at + size]).astype(BF16)


def finish_kernel(parts, *refs):
    *terms, out_ref = refs
    size, hidden = out_ref.shape[0] // parts, out_ref.shape[1] // 2
    for chunk in range(parts):
        keep_a, got_a, keep_b, got_b = terms[4 * chunk : 4 * chunk + 4]
        rows = slice(chunk * size, (chunk + 1) * size)
        out_ref[rows, :hidden] = keep_a[0] + got_a[0].astype(F32)
        out_ref[rows, hidden:] = keep_b[0] + got_b[0].astype(F32)


def call(kernel, out_shapes, scratch, flops, moved, args, specs=None, vmem=24 << 20):
    if specs is not None:
        args = [
            pltpu.with_memory_space_constraint(arg, pltpu.HBM) if spec is HBM else arg
            for arg, spec in zip(args, specs)
        ]
    return pl.pallas_call(
        kernel,
        out_shape=out_shapes,
        in_specs=specs or [VMEM] * len(args),
        out_specs=jax.tree.map(lambda _: VMEM, out_shapes),
        scratch_shapes=scratch,
        compiler_params=pltpu.CompilerParams(vmem_limit_bytes=vmem),
        cost_estimate=pl.CostEstimate(flops=flops, bytes_accessed=moved, transcendentals=0),
    )(*args)


def shape(dims, kind=BF16):
    return jax.ShapeDtypeStruct(dims, kind)


def flip(value, axis, mask):
    size = lax.axis_size(axis)
    return lax.ppermute(value, axis, [(i, i ^ mask) for i in range(size)])


def sum_over_groups(terms, groups, parts):
    bits = groups.bit_length() - 1
    last = []
    for chunk in range(parts):
        send_a, keep_a, send_b, keep_b = terms[4 * chunk : 4 * chunk + 4]
        for step in range(bits):
            got_a = flip(send_a, "group", 1 << step)
            got_b = flip(send_b, "group", 1 << (bits - 1 - step))
            if step == bits - 1:
                last += [keep_a, got_a, keep_b, got_b]
                break
            got_a, got_b = got_a.astype(F32), got_b.astype(F32)
            half = keep_a.shape[0] // 2
            send_a = (keep_a[1::2] + got_a[1::2]).astype(BF16)
            keep_a = keep_a[0::2] + got_a[0::2]
            send_b = (keep_b[half:] + got_b[half:]).astype(BF16)
            keep_b = keep_b[:half] + got_b[:half]
    rows, columns = parts * last[0].shape[1], 2 * last[0].shape[2]
    return call(
        functools.partial(finish_kernel, parts),
        shape((rows, columns), F32),
        [],
        2 * rows * columns,
        10 * rows * columns,
        last,
    )


def term_shapes(groups, width, hidden, parts):
    block = (groups // 2, width // groups // parts, hidden)
    return [shape(block), shape(block, F32), shape(block), shape(block, F32)] * parts


def paired(tokens_in, hidden_grad, routing, weights):
    experts = lax.axis_size("expert")
    groups = lax.axis_size("group")
    rows, width = tokens_in.shape
    hidden = hidden_grad.shape[1]
    joined = width + hidden
    half = experts // 2
    full, low_rows, up_rows = 2 * rows // experts, rows // experts, rows // (2 * experts)
    spill = rows // 4
    slots = half * (full + low_rows + up_rows) + spill
    lane = 128

    select, spilled, own, *pieces = call(
        functools.partial(dispatch_kernel, experts),
        [shape((slots, rows)), shape((spill, joined + lane)), shape((half * up_rows, joined))]
        + [shape((full, joined))] * half
        + [shape((low_rows, joined))] * half,
        [
            pltpu.VMEM((1, rows), jnp.int32),
            pltpu.VMEM((rows, joined), BF16),
            pltpu.SemaphoreType.DMA((3,)),
        ],
        2 * slots * rows * joined,
        2 * slots * joined,
        (routing.reshape(1, rows), tokens_in, hidden_grad),
        specs=[HBM] * 3,
    )
    near, low = pieces[:half], pieces[half:]
    landed = flip(spilled, "group", groups // 2)
    low = [flip(low[k], "expert", half + k) for k in range(half)]
    near = [near[0]] + [flip(near[k], "expert", k) for k in range(1, half)]
    up = call(
        merge_kernel,
        [shape((up_rows, joined))] * half,
        [],
        2 * spill * lane * joined,
        4 * half * up_rows * joined,
        (own, landed),
    )
    up = [flip(up[k], "expert", half + k) for k in range(half)]

    weights = call(
        load_kernel,
        shape(weights.shape),
        [pltpu.SemaphoreType.DMA],
        0,
        weights.size * 2,
        (weights,),
        specs=[HBM],
    )
    names = [f"near{k}" for k in range(half)]
    names += [f"low{k}" for k in range(half)] + [f"up{k}" for k in range(half)]
    arrived = dict(zip(names, [*near, *low, *up]))
    late = [name for name in names if name in LATE]
    early = [name for name in names if name not in LATE]
    early_rows = sum(arrived[name].shape[0] for name in early)
    all_rows = half * (full + low_rows + up_rows)

    def grad_shapes(of):
        return [shape((arrived[name].shape[0], width)) for name in of]

    early_inputs, early_pre, *early_grads = call(
        functools.partial(early_kernel, len(early)),
        [shape((early_rows, width)), shape((early_rows, 2 * hidden))] + grad_shapes(early),
        [],
        8 * early_rows * width * hidden,
        4 * early_rows * joined,
        (*(arrived[name] for name in early), weights),
    )
    out = call(
        functools.partial(late_kernel, groups, PARTS, len(late)),
        grad_shapes(late) + term_shapes(groups, width, hidden, PARTS),
        [pltpu.VMEM((all_rows, width), BF16), pltpu.VMEM((all_rows, 2 * hidden), BF16)],
        4 * (all_rows + 2 * (all_rows - early_rows)) * width * hidden,
        4 * all_rows * joined,
        (early_inputs, early_pre, weights, *(arrived[name] for name in late)),
        vmem=32 << 20,
    )
    terms = out[len(late) :]
    grads = dict(zip(early + late, [*early_grads, *out[: len(late)]]))
    for k in range(half):
        if k:
            grads[f"near{k}"] = flip(grads[f"near{k}"], "expert", k)
        for name in (f"low{k}", f"up{k}"):
            grads[name] = flip(grads[name], "expert", half + k)
    spilled_grad = call(
        split_kernel,
        shape((spill, width)),
        [],
        2 * spill * lane * width,
        4 * half * up_rows * width,
        (landed, *(grads[f"up{k}"] for k in range(half))),
    )
    spilled_grad = flip(spilled_grad, "group", groups // 2)
    weight_grad = sum_over_groups(terms, groups, PARTS)
    tokens_grad = call(
        combine_kernel,
        shape((rows, width)),
        [pltpu.VMEM((slots, width), BF16)],
        2 * slots * rows * width,
        2 * slots * width,
        (select, *(grads[name] for name in names), spilled_grad),
    )
    return tokens_grad, weight_grad


def whole_dispatch_kernel(experts, routing_hbm, tokens_hbm, hidden_hbm, select_ref, out_ref, *rest):
    routing_ref, joined_ref, sems = rest
    copies = load_inputs(routing_hbm, tokens_hbm, hidden_hbm, routing_ref, joined_ref, sems)
    copies[0].wait()
    block = routing_ref[...]
    slots = select_ref.shape[0]
    select = one_hot_rows(block * (slots // experts) + ranks_of(block, experts), slots)
    select_ref[...] = select
    copies[1].wait()
    copies[2].wait()
    for at, size in chunks(out_ref.shape[1], 256):
        columns = slice(at, at + size)
        out_ref[:, columns] = dot(select, joined_ref[:, columns]).astype(BF16)


def whole_expert_kernel(groups, rows_ref, weights_ref, grad_ref, *refs):
    *terms, inputs_ref, pre_ref = refs
    rows_grads([rows_ref], weights_ref, inputs_ref, pre_ref, [grad_ref])
    weight_terms(groups, 1, inputs_ref, pre_ref, terms)


def unpaired(tokens_in, hidden_grad, routing, weights):
    experts = lax.axis_size("expert")
    groups = lax.axis_size("group")
    rows, width = tokens_in.shape
    hidden = hidden_grad.shape[1]
    joined = width + hidden
    capacity = 2 * rows // experts
    slots = experts * capacity

    def exchange(value):
        block = value.reshape(experts, capacity, -1)
        moved = lax.all_to_all(block, "expert", split_axis=0, concat_axis=0, tiled=True)
        return moved.reshape(slots, -1)

    select, outgoing = call(
        functools.partial(whole_dispatch_kernel, experts),
        [shape((slots, rows)), shape((slots, joined))],
        [
            pltpu.VMEM((1, rows), jnp.int32),
            pltpu.VMEM((rows, joined), BF16),
            pltpu.SemaphoreType.DMA((3,)),
        ],
        2 * slots * rows * joined,
        2 * slots * joined,
        (routing.reshape(1, rows), tokens_in, hidden_grad),
        specs=[HBM] * 3,
    )
    grad, *terms = call(
        functools.partial(whole_expert_kernel, groups),
        [shape((slots, width))] + term_shapes(groups, width, hidden, 1),
        [pltpu.VMEM((slots, width), BF16), pltpu.VMEM((slots, 2 * hidden), BF16)],
        12 * slots * width * hidden,
        4 * slots * joined,
        (exchange(outgoing), weights),
        vmem=32 << 20,
    )
    weight_grad = sum_over_groups(terms, groups, 1)
    tokens_grad = call(
        combine_kernel,
        shape((rows, width)),
        [pltpu.VMEM((slots, width), BF16)],
        2 * slots * rows * width,
        2 * slots * width,
        (select, exchange(grad)),
    )
    return tokens_grad, weight_grad


def can_pair(mesh, rows):
    experts, groups = mesh.shape["expert"], mesh.shape["group"]
    return groups % 2 == 0 and rows % (16 * experts) == 0 and experts <= 16


def on_device(pair, tokens_in, hidden_grad, routing, gate_up):
    run = paired if pair else unpaired
    tokens_grad, weight_grad = run(tokens_in, hidden_grad, routing, gate_up[0])
    return (tokens_grad, weight_grad[None])


def solution(mesh):
    devices = mesh.shape["expert"] * mesh.shape["group"]

    def whole(tokens_in, hidden_grad, routing, gate_up):
        pair = can_pair(mesh, routing.shape[0] // devices)
        return jax.shard_map(
            functools.partial(on_device, pair),
            mesh=mesh,
            in_specs=(
                P(("expert", "group"), None),
                P(("expert", "group"), None),
                P(("expert", "group")),
                P("expert", None, None),
            ),
            out_specs=(P(("expert", "group"), None), P("expert", "group", None)),
            check_vma=False,
        )(tokens_in, hidden_grad, routing, gate_up)

    return whole
```

```python
import functools

import jax
import jax.numpy as jnp
from jax import lax
from jax.experimental import pallas as pl
from jax.experimental.pallas import tpu as pltpu
from jax.sharding import PartitionSpec as P


BF16 = jnp.bfloat16
F32 = jnp.float32
MERGE = 20000
LATE = ("low2", "low3", "up0", "up1", "up2", "up3")
VMEM = pl.BlockSpec(memory_space=pltpu.VMEM)
HBM = pl.BlockSpec(memory_space=pltpu.HBM)


def chunks(total, width):
    return [(at, min(width, total - at)) for at in range(0, total, width)]


def dot(a, b):
    return jnp.dot(a, b, preferred_element_type=F32)


def dot_t(a, b):
    return lax.dot_general(a, b, (((0,), (0,)), ((), ())), preferred_element_type=F32)


def dot_nt(a, b):
    return lax.dot_general(a, b, (((1,), (1,)), ((), ())), preferred_element_type=F32)


def stack(pieces, columns=slice(None)):
    if all(piece.shape[0] % 16 == 0 for piece in pieces):
        return jnp.concatenate([piece[:, columns] for piece in pieces], axis=0)
    return jnp.concatenate([piece[:, columns].astype(F32) for piece in pieces], axis=0).astype(BF16)


def unstack(value, pieces, columns):
    start = 0
    for piece in pieces:
        end = start + piece.shape[0]
        piece[:, columns] = value[start:end].astype(BF16)
        start = end


def ranks_of(block, experts):
    rows = block.shape[1]
    one_hot = block == lax.broadcasted_iota(jnp.int32, (experts, rows), 0)
    ones = jnp.where(one_hot, 1.0, 0.0)
    counts = dot(ones.astype(BF16), earlier(rows))
    return jnp.sum(counts * ones, axis=0, keepdims=True).astype(jnp.int32)


def earlier(rows):
    mask = lax.broadcasted_iota(jnp.int32, (rows, rows), 0) < lax.broadcasted_iota(
        jnp.int32, (rows, rows), 1
    )
    return jnp.where(mask, 1.0, 0.0).astype(BF16)


def one_hot_rows(target, count):
    return jnp.where(
        target == lax.broadcasted_iota(jnp.int32, (count, target.shape[1]), 0), 1.0, 0.0
    ).astype(BF16)


def load_inputs(routing_hbm, tokens_hbm, hidden_hbm, routing_ref, joined_ref, sems):
    width = tokens_hbm.shape[1]
    copies = [
        pltpu.make_async_copy(routing_hbm, routing_ref, sems.at[0]),
        pltpu.make_async_copy(tokens_hbm, joined_ref.at[:, :width], sems.at[1]),
        pltpu.make_async_copy(hidden_hbm, joined_ref.at[:, width:], sems.at[2]),
    ]
    for copy in copies:
        copy.start()
    return copies


def input_scratch(rows, width, hidden):
    return [
        pltpu.VMEM((1, rows), jnp.int32),
        pltpu.VMEM((rows, width + hidden), BF16),
        pltpu.SemaphoreType.DMA((3,)),
    ]


def dispatch_kernel(experts, *refs):
    routing_hbm, tokens_hbm, hidden_hbm, select_ref, spill_ref, own_ref, *rest = refs
    near, low = rest[: experts // 2], rest[experts // 2 : experts]
    routing_ref, joined_ref, sems = rest[experts:]
    copies = load_inputs(routing_hbm, tokens_hbm, hidden_hbm, routing_ref, joined_ref, sems)
    rows, joined = joined_ref.shape
    half = experts // 2
    full, low_rows, up_rows = near[0].shape[0], low[0].shape[0], own_ref.shape[0] // half
    low_at = half * full
    own_at = low_at + half * low_rows
    spill_at = own_at + half * up_rows
    kept = low_rows + up_rows
    me = lax.axis_index("expert").astype(jnp.int32)
    copies[0].wait()
    block = routing_ref[...] ^ me
    rank = ranks_of(block, experts)
    far = block - half
    spilled = (far >= 0) & (rank >= kept)
    spilled_ones = jnp.broadcast_to(jnp.where(spilled, 1.0, 0.0), (8, rows)).astype(BF16)
    place = dot(spilled_ones, earlier(rows))[:1].astype(jnp.int32)
    target = jnp.where(
        far < 0,
        block * full + rank,
        jnp.where(
            rank < low_rows,
            low_at + far * low_rows + rank,
            jnp.where(
                spilled, spill_at + place, own_at + far * up_rows + (rank - low_rows)
            ),
        ),
    )
    select = one_hot_rows(target, select_ref.shape[0])
    select_ref[...] = select
    landing = jnp.where(spilled, far * up_rows + (up_rows - 1) - (rank - kept), -1)
    spill_ref[:, joined:] = dot_nt(
        select[spill_at:], one_hot_rows(landing, spill_ref.shape[1] - joined)
    ).astype(BF16)
    copies[1].wait()
    copies[2].wait()
    for at, size in chunks(joined_ref.shape[1], 256):
        columns = slice(at, at + size)
        placed = dot(select, joined_ref[:, columns])
        unstack(placed, [*near, *low, own_ref, spill_ref], columns)


def merge_kernel(own_ref, spill_ref, *piece_refs):
    slots, joined = own_ref.shape
    landing = spill_ref[:, joined:]
    for at, size in chunks(joined, 256):
        columns = slice(at, at + size)
        landed = dot_t(landing, spill_ref[:, columns])[:slots]
        unstack(landed + own_ref[:, columns].astype(F32), piece_refs, columns)


def split_kernel(spill_ref, *refs):
    *pieces, out_ref = refs
    slots = sum(piece.shape[0] for piece in pieces)
    joined = spill_ref.shape[1] - 128
    landing = spill_ref[:, joined:]
    for at, size in chunks(out_ref.shape[1], 512):
        columns = slice(at, at + size)
        value = stack(pieces, columns)
        pad = jnp.zeros((landing.shape[1] - slots, size), BF16)
        out_ref[:, columns] = dot(landing, jnp.concatenate([value, pad], axis=0)).astype(BF16)


def hidden_grads(inputs, cotangent, weights_ref):
    projected = dot(inputs, weights_ref[...])
    hidden = projected.shape[1] // 2
    gate_pre = projected[:, :hidden]
    up_pre = projected[:, hidden:]
    sigmoid_gate = jax.nn.sigmoid(gate_pre)
    gate_grad = cotangent * up_pre * sigmoid_gate * (1.0 + gate_pre * (1.0 - sigmoid_gate))
    up_grad = cotangent * gate_pre * sigmoid_gate
    return jnp.concatenate([gate_grad.astype(BF16), up_grad.astype(BF16)], axis=1)


def input_grads(pre_grad, weights_ref, pieces):
    for at, size in chunks(weights_ref.shape[0], 512):
        columns = slice(at, at + size)
        unstack(dot_nt(pre_grad, weights_ref[columns, :]), pieces, columns)


def rows_hidden(pieces, weights_ref, inputs_ref, pre_ref):
    width = weights_ref.shape[0]
    start = 0
    for run in runs(pieces):
        end = start + sum(piece.shape[0] for piece in run)
        inputs_ref[start:end, :] = stack(run, slice(0, width))
        start = end
    cotangent = jnp.concatenate(
        [stack(run, slice(width, None)).astype(F32) for run in runs(pieces)], axis=0
    )
    pre_ref[...] = hidden_grads(inputs_ref[...], cotangent, weights_ref)


def early_kernel(count, *refs):
    pieces, (weights_ref, inputs_ref, pre_ref), grads = (
        refs[:count],
        refs[count : count + 3],
        refs[count + 3 :],
    )
    rows_hidden(pieces, weights_ref, inputs_ref, pre_ref)
    input_grads(pre_ref[...], weights_ref, grads)


def late_kernel(groups, count, *refs):
    early_inputs_ref, early_pre_ref, weights_ref = refs[:3]
    pieces, (late_pre_ref, *terms) = refs[3 : count + 3], refs[count + 3 : -2]
    inputs_ref, pre_ref = refs[-2:]
    split = early_pre_ref.shape[0]
    inputs_ref[:split, :] = early_inputs_ref[...]
    pre_ref[:split, :] = early_pre_ref[...]
    rows_hidden(pieces, weights_ref, inputs_ref.at[split:, :], late_pre_ref)
    pre_ref[split:, :] = late_pre_ref[...]
    weight_terms(groups, inputs_ref, pre_ref, *terms)


def grads_kernel(pre_ref, weights_ref, *grads):
    input_grads(pre_ref[...], weights_ref, grads)


def weight_terms(groups, inputs_ref, pre_ref, send_a, keep_a, send_b, keep_b):
    me = lax.axis_index("group").astype(jnp.int32)
    part = inputs_ref.shape[1] // groups
    hidden = pre_ref.shape[1] // 2
    pre_grad = pre_ref[...]
    for k in range(groups):
        columns = pl.ds(pl.multiple_of((me ^ k) * part, part), part)
        term = dot_t(inputs_ref[:, columns], pre_grad)
        if k % 2:
            send_a[k // 2] = term[:, :hidden].astype(BF16)
        else:
            keep_a[k // 2] = term[:, :hidden]
        if k >= groups // 2:
            send_b[k - groups // 2] = term[:, hidden:].astype(BF16)
        else:
            keep_b[k] = term[:, hidden:]


def runs(pieces):
    found = []
    for piece in pieces:
        if found and found[-1][0].shape[0] == piece.shape[0]:
            found[-1].append(piece)
        else:
            found.append([piece])
    return found


def last_kernel(count, *refs):
    select_ref, pieces, terms = refs[0], refs[1 : count + 1], refs[count + 1 : count + 5]
    tokens_hbm, weights_hbm, stacked_ref, tokens_ref, weights_ref, sems = refs[count + 5 :]
    copies = []

    def send(source, target, columns):
        copy = pltpu.make_async_copy(
            source.at[:, columns], target.at[:, columns], sems.at[len(copies)]
        )
        copy.start()
        copies.append(copy)

    start = 0
    for run in runs(pieces):
        end = start + sum(piece.shape[0] for piece in run)
        stacked_ref[start:end, :] = stack(run)
        start = end
    hidden = weights_ref.shape[1] // 2
    for at, keep, got in ((0, *terms[:2]), (hidden, *terms[2:])):
        columns = slice(at, at + hidden)
        weights_ref[:, columns] = keep[0] + got[0].astype(F32)
        send(weights_ref, weights_hbm, columns)
    select = select_ref[...]
    for at, size in chunks(tokens_ref.shape[1], 512):
        columns = slice(at, at + size)
        tokens_ref[:, columns] = dot_t(select, stacked_ref[:, columns]).astype(BF16)
        send(tokens_ref, tokens_hbm, columns)
    for copy in copies:
        copy.wait()


def call(kernel, out_shapes, scratch, flops, moved, args, specs=None, outs=VMEM, vmem=24 << 20):
    if specs is not None:
        args = [
            pltpu.with_memory_space_constraint(arg, pltpu.HBM) if spec is HBM else arg
            for arg, spec in zip(args, specs)
        ]
    return pl.pallas_call(
        kernel,
        out_shape=out_shapes,
        in_specs=specs or [VMEM] * len(args),
        out_specs=jax.tree.map(lambda _: outs, out_shapes),
        scratch_shapes=scratch,
        compiler_params=pltpu.CompilerParams(vmem_limit_bytes=vmem),
        cost_estimate=pl.CostEstimate(flops=flops, bytes_accessed=moved, transcendentals=0),
    )(*args)


def shape(dims, kind=BF16):
    return jax.ShapeDtypeStruct(dims, kind)


def flip(value, axis, mask):
    size = lax.axis_size(axis)
    return lax.ppermute(value, axis, [(i, i ^ mask) for i in range(size)])


def sum_over_groups(send_a, keep_a, send_b, keep_b, groups):
    bits = groups.bit_length() - 1
    for step in range(bits):
        got_a = flip(send_a, "group", 1 << step)
        got_b = flip(send_b, "group", 1 << (bits - 1 - step))
        if step < bits - 1:
            got_a, got_b = got_a.astype(F32), got_b.astype(F32)
            half = keep_a.shape[0] // 2
            send_a = (keep_a[1::2] + got_a[1::2]).astype(BF16)
            keep_a = keep_a[0::2] + got_a[0::2]
            send_b = (keep_b[half:] + got_b[half:]).astype(BF16)
            keep_b = keep_b[:half] + got_b[:half]
    return keep_a, got_a, keep_b, got_b


def last(select, pieces, terms, width):
    slots, rows = select.shape
    part, columns = terms[0].shape[1], 2 * terms[0].shape[2]
    return call(
        functools.partial(last_kernel, len(pieces)),
        [shape((rows, width)), shape((part, columns), F32)],
        [
            pltpu.VMEM((slots, width), BF16),
            pltpu.VMEM((rows, width), BF16),
            pltpu.VMEM((part, columns), F32),
            pltpu.SemaphoreType.DMA((2 + len(chunks(width, 512)),)),
        ],
        2 * slots * rows * width,
        2 * slots * width,
        (select, *pieces, *terms),
        outs=HBM,
    )


def term_shapes(groups, width, hidden):
    block = (groups // 2, width // groups, hidden)
    return [shape(block), shape(block, F32), shape(block), shape(block, F32)]


def paired(tokens_in, hidden_grad, routing, weights):
    experts = lax.axis_size("expert")
    groups = lax.axis_size("group")
    rows, width = tokens_in.shape
    hidden = hidden_grad.shape[1]
    joined = width + hidden
    half = experts // 2
    full, low_rows, up_rows = 2 * rows // experts, rows // experts, rows // (2 * experts)
    spill = rows // 4
    slots = half * (full + low_rows + up_rows) + spill
    lane = 128

    select, spilled, own, *pieces = call(
        functools.partial(dispatch_kernel, experts),
        [shape((slots, rows)), shape((spill, joined + lane)), shape((half * up_rows, joined))]
        + [shape((full, joined))] * half
        + [shape((low_rows, joined))] * half,
        input_scratch(rows, width, hidden),
        2 * slots * rows * joined,
        2 * slots * joined,
        (routing.reshape(1, rows), tokens_in, hidden_grad),
        specs=[HBM] * 3,
    )
    near, low = pieces[:half], pieces[half:]
    landed = flip(spilled, "group", groups // 2)
    low = [flip(low[k], "expert", half + k) for k in range(half)]
    near = [near[0]] + [flip(near[k], "expert", k) for k in range(1, half)]
    up = call(
        merge_kernel,
        [shape((up_rows, joined))] * half,
        [],
        MERGE * weights.size,
        4 * half * up_rows * joined,
        (own, landed),
    )
    up = [flip(up[k], "expert", half + k) for k in range(half)]

    names = [f"near{k}" for k in range(half)]
    names += [f"low{k}" for k in range(half)] + [f"up{k}" for k in range(half)]
    arrived = dict(zip(names, [*near, *low, *up]))
    late = [name for name in names if name in LATE]
    early = [name for name in names if name not in LATE]
    early_rows = sum(arrived[name].shape[0] for name in early)
    all_rows = half * (full + low_rows + up_rows)

    def grad_shapes(of):
        return [shape((arrived[name].shape[0], width)) for name in of]

    early_inputs, early_pre, *early_grads = call(
        functools.partial(early_kernel, len(early)),
        [shape((early_rows, width)), shape((early_rows, 2 * hidden))] + grad_shapes(early),
        [],
        8 * early_rows * width * hidden,
        4 * early_rows * joined,
        (*(arrived[name] for name in early), weights),
    )
    late_rows = all_rows - early_rows
    late_pre, *terms = call(
        functools.partial(late_kernel, groups, len(late)),
        [shape((late_rows, 2 * hidden))] + term_shapes(groups, width, hidden),
        [pltpu.VMEM((all_rows, width), BF16), pltpu.VMEM((all_rows, 2 * hidden), BF16)],
        4 * (all_rows + late_rows) * width * hidden,
        4 * all_rows * joined,
        (early_inputs, early_pre, weights, *(arrived[name] for name in late)),
        vmem=32 << 20,
    )
    late_grads = call(
        grads_kernel,
        grad_shapes(late),
        [],
        4 * late_rows * width * hidden,
        4 * late_rows * width,
        (late_pre, weights),
    )
    grads = dict(zip(early + late, [*early_grads, *late_grads]))
    for k in range(half):
        if k:
            grads[f"near{k}"] = flip(grads[f"near{k}"], "expert", k)
        for name in (f"low{k}", f"up{k}"):
            grads[name] = flip(grads[name], "expert", half + k)
    spilled_grad = call(
        split_kernel,
        shape((spill, width)),
        [],
        2 * spill * lane * width,
        4 * half * up_rows * width,
        (landed, *(grads[f"up{k}"] for k in range(half))),
    )
    spilled_grad = flip(spilled_grad, "group", groups // 2)
    pieces = (*(grads[name] for name in names), spilled_grad)
    return last(select, pieces, sum_over_groups(*terms, groups), width)


def whole_dispatch_kernel(experts, routing_hbm, tokens_hbm, hidden_hbm, select_ref, out_ref, *rest):
    routing_ref, joined_ref, sems = rest
    copies = load_inputs(routing_hbm, tokens_hbm, hidden_hbm, routing_ref, joined_ref, sems)
    copies[0].wait()
    block = routing_ref[...]
    slots = select_ref.shape[0]
    select = one_hot_rows(block * (slots // experts) + ranks_of(block, experts), slots)
    select_ref[...] = select
    copies[1].wait()
    copies[2].wait()
    for at, size in chunks(joined_ref.shape[1], 256):
        columns = slice(at, at + size)
        out_ref[:, columns] = dot(select, joined_ref[:, columns]).astype(BF16)


def whole_expert_kernel(groups, rows_ref, weights_ref, grad_ref, *refs):
    *terms, inputs_ref, pre_ref = refs
    rows_hidden([rows_ref], weights_ref, inputs_ref, pre_ref)
    input_grads(pre_ref[...], weights_ref, [grad_ref])
    weight_terms(groups, inputs_ref, pre_ref, *terms)


def unpaired(tokens_in, hidden_grad, routing, weights):
    experts = lax.axis_size("expert")
    groups = lax.axis_size("group")
    rows, width = tokens_in.shape
    hidden = hidden_grad.shape[1]
    joined = width + hidden
    capacity = 2 * rows // experts
    slots = experts * capacity

    def exchange(value):
        block = value.reshape(experts, capacity, -1)
        moved = lax.all_to_all(block, "expert", split_axis=0, concat_axis=0, tiled=True)
        return moved.reshape(slots, -1)

    select, outgoing = call(
        functools.partial(whole_dispatch_kernel, experts),
        [shape((slots, rows)), shape((slots, joined))],
        input_scratch(rows, width, hidden),
        2 * slots * rows * joined,
        2 * slots * joined,
        (routing.reshape(1, rows), tokens_in, hidden_grad),
        specs=[HBM] * 3,
    )
    grad, *terms = call(
        functools.partial(whole_expert_kernel, groups),
        [shape((slots, width))] + term_shapes(groups, width, hidden),
        [pltpu.VMEM((slots, width), BF16), pltpu.VMEM((slots, 2 * hidden), BF16)],
        12 * slots * width * hidden,
        4 * slots * joined,
        (exchange(outgoing), weights),
        vmem=32 << 20,
    )
    return last(select, (exchange(grad),), sum_over_groups(*terms, groups), width)


def can_pair(mesh, rows):
    experts, groups = mesh.shape["expert"], mesh.shape["group"]
    return groups % 2 == 0 and rows % (16 * experts) == 0 and experts <= 16


def on_device(pair, tokens_in, hidden_grad, routing, gate_up):
    run = paired if pair else unpaired
    tokens_grad, weight_grad = run(tokens_in, hidden_grad, routing, gate_up[0])
    return (tokens_grad, weight_grad[None])


def solution(mesh):
    devices = mesh.shape["expert"] * mesh.shape["group"]

    def whole(tokens_in, hidden_grad, routing, gate_up):
        pair = can_pair(mesh, routing.shape[0] // devices)
        return jax.shard_map(
            functools.partial(on_device, pair),
            mesh=mesh,
            in_specs=(
                P(("expert", "group"), None),
                P(("expert", "group"), None),
                P(("expert", "group")),
                P("expert", None, None),
            ),
            out_specs=(P(("expert", "group"), None), P("expert", "group", None)),
            check_vma=False,
        )(tokens_in, hidden_grad, routing, gate_up)

    return whole
```
